32 devices in a mesh: pb: 8 (over z, x), row: 4 (over y, core).
Axes of the slice: x: 2, y: 2, z: 4, core: 2. Of those that a mesh axis runs over, the one named last changes fastest.
Arguments:
- kernels: bfloat16 [8, 4096, 4096], P('pb', 'row'), may hold values from -6 to 6
- orbitals: bfloat16 [4096, 1024], P('pb'), may hold values from -0.75 to 0.75
- pairs: int32 [8, 4, 2], replicated, may hold values from 0 to 15
- k_slot: int32 [16], replicated, may hold values from 0 to 15, each once
- pair_count: int32 [8], replicated, may hold values from 1 to 4, as said below
Outputs:
- exchange_fields: float32 [4, 1024, 1024], P('row', 'pb')
The draws below stay inside these ranges and needn't reach their ends.
Inputs may be any that keep to these rules, and one draw needn't show every extreme that they name: `k_slot`: every slot holds exactly one k-point. pairs p < pair_count[q] are live; some transfer vector has all 4 live.
All inputs are finite; a program needn't handle non-finite values.
Results may differ from the reference program's by a relative error of at most 0.0029.
Values may be sent and summed in bfloat16 or wider, within the bound.
A program may use at most 128 MiB of HBM per device.

```python
import jax
import jax.numpy as jnp
from jax import lax

NMU = 4096
NORB = 64
NPAIR = 4
Q = 8
K = 16
N_ROW = 4


def draw_pair_count(key, part):
    first_key = jax.random.fold_in(key, 11)
    second_key = jax.random.fold_in(key, 23)
    counts = jax.random.randint(first_key, (Q,), 1, NPAIR + 1).astype(jnp.int32)
    full_index = jax.random.randint(second_key, (), 0, Q)
    return counts.at[full_index].set(NPAIR).astype(jnp.int32)


def place_ends(entries, key, low, top_value):
    index_at = [jax.random.randint(jax.random.fold_in(key, axis), (), 0, length) for axis, length in enumerate(entries.shape)]
    widest = entries.shape.index(max(entries.shape))
    beside = index_at[:widest] + [(index_at[widest] + 1) % entries.shape[widest]] + index_at[widest + 1:]
    return entries.at[tuple(index_at)].set(low).at[tuple(beside)].set(top_value)


def block_levels(stream_key, shape, split, smallest, high):
    factor_of, own = 1.0, jax.random.fold_in(stream_key, 6)
    for axis_at, blocks in split:
        heights = jnp.exp(jax.random.uniform(jax.random.fold_in(own, axis_at), (blocks,), jnp.float32, smallest / len(split), high / len(split)))
        factor_of = factor_of * jnp.repeat(heights, shape[axis_at] // blocks).reshape([-1 if axis == axis_at else 1 for axis in range(len(shape))])
    return factor_of


def scatter_about(own_key, dims, width, reach, cuts=(), held_as=jnp.bfloat16):
    drawn = jax.random.normal(own_key, dims, jnp.float32) * width
    if len(cuts) > 0:
        drawn = block_levels(own_key, dims, cuts, -0.22, 0.18) * drawn
    return jnp.clip(drawn, min=-reach, max=reach).astype(held_as)


def setup_inputs(seed: int = 0) -> dict:
    key_list = jax.random.split(jax.random.key(seed), 6)
    kernels = scatter_about(key_list[0], (Q, NMU, NMU), 1.0, 6.0, ((0, 8), (1, 4)))
    orbitals = scatter_about(key_list[1], (NMU, K * NORB), 0.125, 0.75, ((0, 8),))
    pairs = place_ends(jax.random.randint(key_list[2], (Q, NPAIR, 2), 0, K), jax.random.fold_in(key_list[2], 1), 0, K - 1).astype(jnp.int32)
    k_slot = jax.random.permutation(key_list[3], K).astype(jnp.int32)
    pair_count = draw_pair_count(jax.random.fold_in(key_list[5], 71), 0)
    return {"kernels": kernels, "orbitals": orbitals, "pairs": pairs, "k_slot": k_slot, "pair_count": pair_count}


def pair_fields(weight, orb_left, orb_right):
    wide_weight = weight.astype(jnp.float32)
    right_gram = jnp.dot(orb_right, orb_right.T, preferred_element_type=jnp.float32)
    first_term = jnp.dot((wide_weight * right_gram).astype(jnp.bfloat16), orb_left, preferred_element_type=jnp.float32)
    left_gram = jnp.dot(orb_left, orb_left.T, preferred_element_type=jnp.float32)
    second_hadamard = (wide_weight * left_gram).astype(jnp.bfloat16)
    second_term = jnp.dot(second_hadamard.T, orb_right, preferred_element_type=jnp.float32)
    return first_term, second_term


def reference(kernels, orbitals, pairs, k_slot, pair_count):
    orbital_cube = orbitals.reshape(NMU, K, NORB)

    def per_vector(field_sum, inputs):
        weight, pair_list, live_count = inputs
        for pair_index in range(NPAIR):
            k_left = pair_list[pair_index, 0]
            k_right = pair_list[pair_index, 1]
            orb_left = orbital_cube[:, k_slot[k_left], :]
            orb_right = orbital_cube[:, k_slot[k_right], :]
            first_term, second_term = pair_fields(weight, orb_left, orb_right)
            live_flag = jnp.where(pair_index < live_count, 1.0, 0.0).astype(jnp.float32)
            field_sum = field_sum.at[:, k_left, :].add(live_flag * first_term)
            field_sum = field_sum.at[:, k_right, :].add(live_flag * second_term)
        return field_sum, None

    start_sum = jnp.zeros((NMU, K, NORB), jnp.float32)
    field_sum, unused = lax.scan(per_vector, start_sum, (kernels, pairs, pair_count))
    return field_sum.reshape(N_ROW, NMU // N_ROW, K * NORB)
```

```python
import functools

import jax
import jax.numpy as jnp
from jax import lax
from jax.experimental import pallas as pl
from jax.experimental.pallas import tpu as pltpu
from jax.sharding import PartitionSpec as P

MESH = pl.DeviceIdType.MESH
BF16 = jnp.bfloat16
F32 = jnp.float32
NT = (((1,), (1,)), ((), ()))


def pick_kernel(width, pairs_ref, slot_ref, orb_ref, out_ref):
    pair_total, pb_count, half, lanes = out_ref.shape
    part = lax.rem(lax.axis_index("row"), 2)
    rows = pl.ds(pl.multiple_of(part * half, half), half)
    low = lax.broadcasted_iota(jnp.int32, (half, lanes), 1) < width

    def fetch(k, want):
        slot = slot_ref[k]
        block = orb_ref[rows, pl.ds(pl.multiple_of((slot >> 1) * lanes, lanes), lanes)].astype(F32)
        moved = pltpu.roll(block, width, 1)
        return jnp.where((slot & 1) == want, block, moved)

    def step(n, carry):
        q, p = lax.rem(n, pb_count), lax.div(n, pb_count)
        left = fetch(pairs_ref[q, p, 0], 0)
        right = fetch(pairs_ref[q, p, 1], 1)
        out_ref[p, q] = jnp.where(low, left, right).astype(BF16)
        return carry

    lax.fori_loop(0, pair_total * pb_count, step, 0)


def main_kernel(dims, picked, kern, out, w, basis, rows_r, rows_l, rows_t, f1, f2s, f2r, cbuf,
                w_sem, d_send, d_recv, g_send, g_recv, s_send, s_recv, c_send, c_recv):
    pb_count, row_devices, pair_total, half, tile, width = dims
    pb, row = lax.axis_index("pb"), lax.axis_index("row")
    part = lax.rem(row, 2)
    mate = row + 1 - 2 * part
    row_count, point_total = w.shape
    lanes = basis.shape[2]
    share = row_count // pb_count
    tiles = point_total // tile
    per_chunk = row_count // tile

    w_copy = pltpu.make_async_copy(kern.at[0], w, w_sem)
    w_copy.start()

    barrier = pltpu.get_barrier_semaphore()

    def greet_pb(d, c):
        pl.semaphore_signal(barrier, inc=1, device_id=(lax.rem(pb + d, pb_count), row), device_id_type=MESH)
        return c

    def greet_row(d, c):
        pl.semaphore_signal(barrier, inc=1, device_id=(pb, lax.rem(row + d, row_devices)), device_id_type=MESH)
        return c

    lax.fori_loop(1, pb_count, greet_pb, 0)
    lax.fori_loop(1, row_devices, greet_row, 0)
    pl.semaphore_wait(barrier, pb_count + row_devices - 2)

    def block_rows(j, which):
        return pl.ds(pl.multiple_of((j * 2 + which) * half, half), half)

    def own(p):
        return pltpu.make_async_copy(picked.at[p, pb], basis.at[p, block_rows(pb, part)], d_recv.at[p, 0])

    def direct(p, d):
        q = lax.rem(pb + d, pb_count)
        return pltpu.make_async_remote_copy(
            src_ref=picked.at[p, q], dst_ref=basis.at[p, block_rows(pb, part)],
            send_sem=d_send.at[p, d], recv_sem=d_recv.at[p, d],
            device_id=(q, row), device_id_type=MESH)

    def relay(p, d):
        j = lax.rem(pb + pb_count - d, pb_count)
        spot = basis.at[p, block_rows(j, part)]
        return pltpu.make_async_remote_copy(
            src_ref=spot, dst_ref=spot, send_sem=g_send.at[p, d], recv_sem=g_recv.at[p, d],
            device_id=(pb, mate), device_id_type=MESH)

    def shed(p, d):
        to = lax.rem(row + d, row_devices)
        return pltpu.make_async_remote_copy(
            src_ref=f2s.at[p, to], dst_ref=f2r.at[p, d], send_sem=s_send.at[p, d], recv_sem=s_recv.at[p, d],
            device_id=(pb, to), device_id_type=MESH)

    def c_rows(j):
        return pl.ds(pl.multiple_of(j * share, share), share)

    def own_c(p):
        return pltpu.make_async_copy(cbuf.at[p, c_rows(pb)], out.at[p, pb], c_recv.at[p, 0])

    def give(p, d):
        j = lax.rem(pb + d, pb_count)
        return pltpu.make_async_remote_copy(
            src_ref=cbuf.at[p, c_rows(j)], dst_ref=out.at[p, pb], send_sem=c_send.at[p, d], recv_sem=c_recv.at[p, d],
            device_id=(j, row), device_id_type=MESH)

    def loop(low, high, body):
        def step(i, c):
            body(i)
            return c
        lax.fori_loop(low, high, step, 0)

    def send_pair(p):
        own(p).start()
        loop(1, pb_count, lambda d: direct(p, d).start())

    loop(0, pair_total, send_pair)

    def relay_pair(p):
        own(p).wait()
        relay(p, 0).start()

        def one(d):
            direct(p, d).wait_recv()
            relay(p, d).start()

        loop(1, pb_count, one)

    low = lax.broadcasted_iota(jnp.int32, (row_count, lanes), 1) < width

    def finish_pair(p):
        total = f2s[p, row].astype(F32)
        for d in range(1, row_devices):
            shed(p, d).wait_recv()
            total = total + f2r[p, d].astype(F32)
        stacked = jnp.concatenate([jnp.zeros_like(total), total], axis=0)
        cbuf[p] = jnp.where(low, f1[p], stacked.T).astype(BF16)
        own_c(p).start()
        loop(1, pb_count, lambda d: give(p, d).start())

    def tiles_of(p, start, stop):
        def one(t):
            cols = pl.ds(pl.multiple_of(t * tile, tile), tile)
            there = basis[p, cols, :]
            second = None
            chunk = row_count // 2
            for m in range(2):
                here = slice(m * chunk, (m + 1) * chunk)
                weight = w[here, cols].astype(F32)
                gram = lax.dot_general(rows_r[here], there, NT, preferred_element_type=F32)
                f1[p, here] += jnp.dot((weight * gram).astype(BF16), there, preferred_element_type=F32)
                gram = lax.dot_general(rows_l[here], there, NT, preferred_element_type=F32)
                term = jnp.dot(rows_t[:, here], (weight * gram).astype(BF16), preferred_element_type=F32)
                second = term if second is None else second + term
            inner = pl.ds(pl.multiple_of(lax.rem(t, per_chunk) * tile, tile), tile)
            f2s[p, lax.div(t, per_chunk), :, inner] = second[width:].astype(BF16)

        loop(start, stop, one)

    relay_pair(0)
    w_copy.wait()

    def pair_step(p):
        loop(0, pb_count, lambda d: relay(p, d).wait_recv())
        mine = basis[p, pl.ds(pl.multiple_of(row * row_count, row_count), row_count), :]
        rows_r[...] = jnp.where(low, 0, mine.astype(F32)).astype(BF16)
        rows_l[...] = jnp.where(low, mine.astype(F32), 0).astype(BF16)
        rows_t[...] = mine.astype(F32).T.astype(BF16)
        f1[p] = jnp.zeros((row_count, lanes), F32)
        tiles_of(p, 0, tiles // 2)

        @pl.when(p + 1 < pair_total)
        def _():
            relay_pair(p + 1)

        @pl.when(p > 0)
        def _():
            finish_pair(p - 1)

        tiles_of(p, tiles // 2, tiles)
        loop(1, row_devices, lambda d: shed(p, d).start())

    loop(0, pair_total, pair_step)
    finish_pair(pair_total - 1)

    def settle(p):
        own_c(p).wait()
        relay(p, 0).wait_send()

        def one(d):
            direct(p, d).wait_send()
            relay(p, d).wait_send()
            give(p, d).wait()

        loop(1, pb_count, one)
        loop(1, row_devices, lambda d: shed(p, d).wait_send())

    loop(0, pair_total, settle)


def combine_kernel(width, pairs_ref, count_ref, got_ref, out_ref):
    pair_total, pb_count, share, lanes = got_ref.shape
    low = lax.broadcasted_iota(jnp.int32, (share, lanes), 1) < width
    out_ref[...] = jnp.zeros_like(out_ref)

    def step(n, carry):
        q, p = lax.rem(n, pb_count), lax.div(n, pb_count)

        @pl.when(p < count_ref[q])
        def _():
            block = got_ref[p, q].astype(F32)
            moved = pltpu.roll(block, width, 1)
            for side in range(2):
                k = pairs_ref[q, p, side]
                odd = k & 1
                value = jnp.where(odd == side, block, moved)
                value = jnp.where(low == (odd == 0), value, 0.0)
                spot = pl.ds(pl.multiple_of((k >> 1) * lanes, lanes), lanes)
                out_ref[0, :, spot] += value

        return carry

    lax.fori_loop(0, pair_total * pb_count, step, 0)


def shards(kernels, orbitals, pairs, k_slot, pair_count):
    pb_count, row_devices = lax.axis_size("pb"), lax.axis_size("row")
    row_count, point_total = kernels.shape[1:]
    pair_total = pairs.shape[1]
    k_total = k_slot.shape[0]
    width = orbitals.shape[1] // k_total
    lanes = 2 * width
    half = orbitals.shape[0] // 2
    share = row_count // pb_count
    tile = row_count // 2
    smem = pl.BlockSpec(memory_space=pltpu.SMEM)
    vmem = pl.BlockSpec(memory_space=pltpu.VMEM)
    hbm = pl.BlockSpec(memory_space=pl.ANY)
    picked = pl.pallas_call(
        functools.partial(pick_kernel, width),
        out_shape=jax.ShapeDtypeStruct((pair_total, pb_count, half, lanes), BF16),
        in_specs=[smem, smem, vmem],
        out_specs=vmem,
    )(pairs, k_slot, orbitals)
    sems = pltpu.SemaphoreType.DMA
    got = pl.pallas_call(
        functools.partial(main_kernel, (pb_count, row_devices, pair_total, half, tile, width)),
        out_shape=jax.ShapeDtypeStruct((pair_total, pb_count, share, lanes), BF16),
        in_specs=[hbm, hbm],
        out_specs=hbm,
        scratch_shapes=[
            pltpu.VMEM((row_count, point_total), BF16),
            pltpu.VMEM((pair_total, point_total, lanes), BF16),
            pltpu.VMEM((row_count, lanes), BF16),
            pltpu.VMEM((row_count, lanes), BF16),
            pltpu.VMEM((lanes, row_count), BF16),
            pltpu.VMEM((pair_total, row_count, lanes), F32),
            pltpu.VMEM((pair_total, row_devices, width, row_count), BF16),
            pltpu.VMEM((pair_total, row_devices, width, row_count), BF16),
            pltpu.VMEM((pair_total, row_count, lanes), BF16),
            sems,
            sems((pair_total, pb_count)),
            sems((pair_total, pb_count)),
            sems((pair_total, pb_count)),
            sems((pair_total, pb_count)),
            sems((pair_total, row_devices)),
            sems((pair_total, row_devices)),
            sems((pair_total, pb_count)),
            sems((pair_total, pb_count)),
        ],
        compiler_params=pltpu.CompilerParams(
            collective_id=0, has_side_effects=True, vmem_limit_bytes=56 * 1024 * 1024
        ),
    )(picked, kernels)
    return pl.pallas_call(
        functools.partial(combine_kernel, width),
        out_shape=jax.ShapeDtypeStruct((1, share, k_total * width), F32),
        in_specs=[smem, smem, vmem],
        out_specs=vmem,
    )(pairs, pair_count, got)


def solution(mesh):
    placed = (P("pb", "row", None), P("pb", None), P(), P(), P())
    return jax.shard_map(
        shards, mesh=mesh, in_specs=placed, out_specs=P("row", "pb", None), check_vma=False
    )
```

```python
import functools

import jax
import jax.numpy as jnp
from jax import lax
from jax.experimental import pallas as pl
from jax.experimental.pallas import tpu as pltpu
from jax.sharding import PartitionSpec as P

MESH = pl.DeviceIdType.MESH
BF16 = jnp.bfloat16
F32 = jnp.float32
NT = (((1,), (1,)), ((), ()))


def pick_kernel(width, pairs_ref, slot_ref, orb_ref, out_ref):
    pair_total, pb_count, piece, lanes = out_ref.shape
    rows = pl.ds(pl.multiple_of(lax.axis_index("row") * piece, piece), piece)
    low = lax.broadcasted_iota(jnp.int32, (piece, lanes), 1) < width

    def fetch(k, want):
        slot = slot_ref[k]
        block = orb_ref[rows, pl.ds(pl.multiple_of((slot >> 1) * lanes, lanes), lanes)].astype(F32)
        moved = pltpu.roll(block, width, 1)
        return jnp.where((slot & 1) == want, block, moved)

    def step(n, carry):
        q, p = lax.rem(n, pb_count), lax.div(n, pb_count)
        left = fetch(pairs_ref[q, p, 0], 0)
        right = fetch(pairs_ref[q, p, 1], 1)
        out_ref[p, q] = jnp.where(low, left, right).astype(BF16)
        return carry

    lax.fori_loop(0, pair_total * pb_count, step, 0)


def main_kernel(dims, picked, kern, out, w, basis, rows_r, rows_l, rows_t, f1, f2s, f2r, cbuf,
                w_sem, d_send, d_recv, g_send, g_recv, h_send, h_recv, y_send, y_recv,
                s_send, s_recv, c_send, c_recv):
    pb_count, row_devices, pair_total, piece, width = dims
    pb, row = lax.axis_index("pb"), lax.axis_index("row")
    chips = row_devices // 2
    part, chip = lax.rem(row, 2), lax.div(row, 2)
    mate = row + 1 - 2 * part
    row_count = w.shape[0]
    lanes = basis.shape[2]
    share = row_count // pb_count
    order = [(e, flip) for e in range(1, chips) for flip in (0, 1)] + [(0, 1), (0, 0)]

    def peer(e, flip):
        side = 1 - part if flip else part
        return 2 * lax.rem(chip + e, chips) + side

    w_copy = pltpu.make_async_copy(kern.at[0], w, w_sem)
    w_copy.start()

    barrier = pltpu.get_barrier_semaphore()

    def greet_pb(d, c):
        pl.semaphore_signal(barrier, inc=1, device_id=(lax.rem(pb + d, pb_count), row), device_id_type=MESH)
        return c

    def greet_row(d, c):
        pl.semaphore_signal(barrier, inc=1, device_id=(pb, lax.rem(row + d, row_devices)), device_id_type=MESH)
        return c

    lax.fori_loop(1, pb_count, greet_pb, 0)
    lax.fori_loop(1, row_devices, greet_row, 0)
    pl.semaphore_wait(barrier, pb_count + row_devices - 2)

    def spot(p, j, which):
        return basis.at[p, pl.ds(pl.multiple_of((j * row_devices + which) * piece, piece), piece)]

    def source(d):
        return lax.rem(pb + pb_count - d, pb_count)

    def own(p):
        return pltpu.make_async_copy(picked.at[p, pb], spot(p, pb, row), d_recv.at[p, 0])

    def direct(p, d):
        q = lax.rem(pb + d, pb_count)
        return pltpu.make_async_remote_copy(
            src_ref=picked.at[p, q], dst_ref=spot(p, pb, row),
            send_sem=d_send.at[p, d], recv_sem=d_recv.at[p, d],
            device_id=(q, row), device_id_type=MESH)

    def across(p, e, d):
        block = spot(p, source(d), row)
        return pltpu.make_async_remote_copy(
            src_ref=block, dst_ref=block, send_sem=y_send.at[p, e - 1, d], recv_sem=y_recv.at[p, e - 1, d],
            device_id=(pb, peer(e, 0)), device_id_type=MESH)

    def to_mate(p, d):
        block = spot(p, source(d), row)
        return pltpu.make_async_remote_copy(
            src_ref=block, dst_ref=block, send_sem=g_send.at[p, d], recv_sem=g_recv.at[p, d],
            device_id=(pb, mate), device_id_type=MESH)

    def onward(p, e, d):
        block = spot(p, source(d), peer(chips - e, 0))
        return pltpu.make_async_remote_copy(
            src_ref=block, dst_ref=block, send_sem=h_send.at[p, e - 1, d], recv_sem=h_recv.at[p, e - 1, d],
            device_id=(pb, mate), device_id_type=MESH)

    def shed(p, s):
        to = peer(*order[s])
        return pltpu.make_async_remote_copy(
            src_ref=f2s.at[p, s], dst_ref=f2r.at[p, s], send_sem=s_send.at[p, s], recv_sem=s_recv.at[p, s],
            device_id=(pb, to), device_id_type=MESH)

    def c_rows(j):
        return pl.ds(pl.multiple_of(j * share, share), share)

    def own_c(p):
        return pltpu.make_async_copy(cbuf.at[p, c_rows(pb)], out.at[p, pb], c_recv.at[p, 0])

    def give(p, d):
        j = lax.rem(pb + d, pb_count)
        return pltpu.make_async_remote_copy(
            src_ref=cbuf.at[p, c_rows(j)], dst_ref=out.at[p, pb], send_sem=c_send.at[p, d], recv_sem=c_recv.at[p, d],
            device_id=(j, row), device_id_type=MESH)

    def loop(low, high, body):
        def step(i, c):
            body(i)
            return c
        lax.fori_loop(low, high, step, 0)

    def send_pair(p):
        own(p).start()
        loop(1, pb_count, lambda d: direct(p, d).start())

    loop(0, pair_total, send_pair)

    def spread(p):
        def pass_on(d):
            for e in range(1, chips):
                across(p, e, d).start()
            to_mate(p, d).start()

        own(p).wait()
        pass_on(0)

        def one(d):
            direct(p, d).wait_recv()
            pass_on(d)

        loop(1, pb_count, one)

    def pass_far(p):
        for e in range(1, chips):
            def one(d):
                across(p, e, d).wait_recv()
                onward(p, e, d).start()

            loop(0, pb_count, one)

    low = lax.broadcasted_iota(jnp.int32, (row_count, lanes), 1) < width

    def finish_pair(p):
        total = f2s[p, row_devices - 1].astype(F32)
        for s in range(row_devices - 1):
            shed(p, s).wait_recv()
            total = total + f2r[p, s].astype(F32)
        stacked = jnp.concatenate([jnp.zeros_like(total), total], axis=0)
        cbuf[p] = jnp.where(low, f1[p], stacked.T).astype(BF16)
        loop(1, pb_count, lambda d: give(p, d).start())
        own_c(p).start()

    def tile_of(p, s):
        cols = pl.ds(pl.multiple_of(peer(*order[s]) * row_count, row_count), row_count)
        there = basis[p, cols, :]
        second = None
        chunk = row_count // 2
        for m in range(2):
            here = slice(m * chunk, (m + 1) * chunk)
            weight = w[here, cols].astype(F32)
            gram = lax.dot_general(rows_r[here], there, NT, preferred_element_type=F32)
            first = jnp.dot((weight * gram).astype(BF16), there, preferred_element_type=F32)
            f1[p, here] = first if s == 0 else f1[p, here] + first
            gram = lax.dot_general(rows_l[here], there, NT, preferred_element_type=F32)
            term = jnp.dot(rows_t[:, here], (weight * gram).astype(BF16), preferred_element_type=F32)
            second = term if second is None else second + term
        f2s[p, s] = second[width:].astype(BF16)
        if s < row_devices - 1:
            shed(p, s).start()

    spread(0)
    pass_far(0)
    w_copy.wait()

    def pair_step(p):
        def arrive(d):
            to_mate(p, d).wait_recv()
            for e in range(1, chips):
                onward(p, e, d).wait_recv()

        loop(0, pb_count, arrive)
        mine = basis[p, pl.ds(pl.multiple_of(row * row_count, row_count), row_count), :].astype(F32)
        rows_r[...] = jnp.where(low, 0, mine).astype(BF16)
        rows_l[...] = jnp.where(low, mine, 0).astype(BF16)
        rows_t[...] = mine.T.astype(BF16)
        for s in range(row_devices):
            tile_of(p, s)
            if s == 0:
                pl.when(p + 1 < pair_total)(lambda: spread(p + 1))
                pl.when(p > 0)(lambda: finish_pair(p - 1))
            if s == row_devices - 2:
                pl.when(p + 1 < pair_total)(lambda: pass_far(p + 1))

    loop(0, pair_total, pair_step)
    finish_pair(pair_total - 1)

    def settle(p):
        own_c(p).wait()

        def relayed(d):
            to_mate(p, d).wait_send()
            for e in range(1, chips):
                across(p, e, d).wait_send()
                onward(p, e, d).wait_send()

        loop(0, pb_count, relayed)

        def one(d):
            direct(p, d).wait_send()
            give(p, d).wait()

        loop(1, pb_count, one)
        for s in range(row_devices - 1):
            shed(p, s).wait_send()

    loop(0, pair_total, settle)


def combine_kernel(width, pairs_ref, count_ref, got_ref, out_ref):
    pair_total, pb_count, share, lanes = got_ref.shape
    low = lax.broadcasted_iota(jnp.int32, (share, lanes), 1) < width
    out_ref[...] = jnp.zeros_like(out_ref)

    def step(n, carry):
        q, p = lax.rem(n, pb_count), lax.div(n, pb_count)

        @pl.when(p < count_ref[q])
        def _():
            block = got_ref[p, q].astype(F32)
            moved = pltpu.roll(block, width, 1)
            for side in range(2):
                k = pairs_ref[q, p, side]
                odd = k & 1
                value = jnp.where(odd == side, block, moved)
                value = jnp.where(low == (odd == 0), value, 0.0)
                spot = pl.ds(pl.multiple_of((k >> 1) * lanes, lanes), lanes)
                out_ref[0, :, spot] += value

        return carry

    lax.fori_loop(0, pair_total * pb_count, step, 0)


def shards(kernels, orbitals, pairs, k_slot, pair_count):
    pb_count, row_devices = lax.axis_size("pb"), lax.axis_size("row")
    row_count, point_total = kernels.shape[1:]
    pair_total = pairs.shape[1]
    k_total = k_slot.shape[0]
    width = orbitals.shape[1] // k_total
    lanes = 2 * width
    piece = orbitals.shape[0] // row_devices
    far = max(row_devices // 2 - 1, 1)
    share = row_count // pb_count
    smem = pl.BlockSpec(memory_space=pltpu.SMEM)
    vmem = pl.BlockSpec(memory_space=pltpu.VMEM)
    hbm = pl.BlockSpec(memory_space=pl.ANY)
    picked = pl.pallas_call(
        functools.partial(pick_kernel, width),
        out_shape=jax.ShapeDtypeStruct((pair_total, pb_count, piece, lanes), BF16),
        in_specs=[smem, smem, vmem],
        out_specs=vmem,
    )(pairs, k_slot, orbitals)
    sems = pltpu.SemaphoreType.DMA
    got = pl.pallas_call(
        functools.partial(main_kernel, (pb_count, row_devices, pair_total, piece, width)),
        out_shape=jax.ShapeDtypeStruct((pair_total, pb_count, share, lanes), BF16),
        in_specs=[hbm, hbm],
        out_specs=hbm,
        scratch_shapes=[
            pltpu.VMEM((row_count, point_total), BF16),
            pltpu.VMEM((pair_total, point_total, lanes), BF16),
            pltpu.VMEM((row_count, lanes), BF16),
            pltpu.VMEM((row_count, lanes), BF16),
            pltpu.VMEM((lanes, row_count), BF16),
            pltpu.VMEM((pair_total, row_count, lanes), F32),
            pltpu.VMEM((pair_total, row_devices, width, row_count), BF16),
            pltpu.VMEM((pair_total, row_devices, width, row_count), BF16),
            pltpu.VMEM((pair_total, row_count, lanes), BF16),
            sems,
            sems((pair_total, pb_count)),
            sems((pair_total, pb_count)),
            sems((pair_total, pb_count)),
            sems((pair_total, pb_count)),
            sems((pair_total, far, pb_count)),
            sems((pair_total, far, pb_count)),
            sems((pair_total, far, pb_count)),
            sems((pair_total, far, pb_count)),
            sems((pair_total, row_devices)),
            sems((pair_total, row_devices)),
            sems((pair_total, pb_count)),
            sems((pair_total, pb_count)),
        ],
        compiler_params=pltpu.CompilerParams(
            collective_id=0, has_side_effects=True, vmem_limit_bytes=56 * 1024 * 1024
        ),
    )(picked, kernels)
    return pl.pallas_call(
        functools.partial(combine_kernel, width),
        out_shape=jax.ShapeDtypeStruct((1, share, k_total * width), F32),
        in_specs=[smem, smem, vmem],
        out_specs=vmem,
    )(pairs, pair_count, got)


def solution(mesh):
    placed = (P("pb", "row", None), P("pb", None), P(), P(), P())
    return jax.shard_map(
        shards, mesh=mesh, in_specs=placed, out_specs=P("row", "pb", None), check_vma=False
    )
```

```python
import functools

import jax
import jax.numpy as jnp
from jax import lax
from jax.experimental import pallas as pl
from jax.experimental.pallas import tpu as pltpu
from jax.sharding import PartitionSpec as P

MESH = pl.DeviceIdType.MESH
BF16 = jnp.bfloat16
F32 = jnp.float32
NT = (((1,), (1,)), ((), ()))


def pick_kernel(width, pairs_ref, slot_ref, orb_ref, out_ref):
    pair_total, pb_count, piece, lanes = out_ref.shape
    rows = pl.ds(pl.multiple_of(lax.axis_index("row") * piece, piece), piece)
    low = lax.broadcasted_iota(jnp.int32, (piece, lanes), 1) < width

    def fetch(k, want):
        slot = slot_ref[k]
        block = orb_ref[rows, pl.ds(pl.multiple_of((slot >> 1) * lanes, lanes), lanes)].astype(F32)
        moved = pltpu.roll(block, width, 1)
        return jnp.where((slot & 1) == want, block, moved)

    def step(q, carry):
        for p in range(pair_total):
            left = fetch(pairs_ref[q, p, 0], 0)
            right = fetch(pairs_ref[q, p, 1], 1)
            out_ref[p, q] = jnp.where(low, left, right).astype(BF16)
        return carry

    lax.fori_loop(0, pb_count, step, 0)


def main_kernel(dims, picked, kern, out, w, basis, rows_r, rows_l, rows_t, f1, f2s, f2r, cbuf,
                w_sem, d_send, d_recv, g_send, g_recv, h_send, h_recv, y_send, y_recv,
                s_send, s_recv, c_send, c_recv):
    pb_count, row_devices, pair_total, piece, width = dims
    pb, row = lax.axis_index("pb"), lax.axis_index("row")
    chips = row_devices // 2
    part, chip = lax.rem(row, 2), lax.div(row, 2)
    mate = row + 1 - 2 * part
    row_count = w.shape[0]
    lanes = basis.shape[4]
    share = row_count // pb_count
    order = [(e, flip) for e in range(1, chips) for flip in (0, 1)] + [(0, 1), (0, 0)]

    def peer(e, flip):
        side = 1 - part if flip else part
        return 2 * lax.rem(chip + e, chips) + side

    w_copy = pltpu.make_async_copy(kern.at[0], w, w_sem)
    w_copy.start()

    barrier = pltpu.get_barrier_semaphore()

    def greet_pb(d, c):
        pl.semaphore_signal(barrier, inc=1, device_id=(lax.rem(pb + d, pb_count), row), device_id_type=MESH)
        return c

    def greet_row(d, c):
        pl.semaphore_signal(barrier, inc=1, device_id=(pb, lax.rem(row + d, row_devices)), device_id_type=MESH)
        return c

    lax.fori_loop(1, pb_count, greet_pb, 0)
    lax.fori_loop(1, row_devices, greet_row, 0)
    pl.semaphore_wait(barrier, pb_count + row_devices - 2)

    def spot(p, j, which):
        return basis.at[p, j, which]

    def points(p, r):
        span = pb_count // row_devices
        return basis[p, pl.ds(r * span, span)].reshape(row_count, lanes)

    def own(p):
        return pltpu.make_async_copy(picked.at[p, pb], spot(p, pb, row), d_recv.at[p, 0])

    def direct(p, d):
        q = lax.rem(pb + d, pb_count)
        return pltpu.make_async_remote_copy(
            src_ref=picked.at[p, q], dst_ref=spot(p, pb, row),
            send_sem=d_send.at[p, d], recv_sem=d_recv.at[p, d],
            device_id=(q, row), device_id_type=MESH)

    def across(p, e):
        block = basis.at[p, :, row]
        return pltpu.make_async_remote_copy(
            src_ref=block, dst_ref=block, send_sem=y_send.at[p, e - 1], recv_sem=y_recv.at[p, e - 1],
            device_id=(pb, peer(e, 0)), device_id_type=MESH)

    def to_mate(p):
        block = basis.at[p, :, row]
        return pltpu.make_async_remote_copy(
            src_ref=block, dst_ref=block, send_sem=g_send.at[p], recv_sem=g_recv.at[p],
            device_id=(pb, mate), device_id_type=MESH)

    def onward(p, e):
        block = basis.at[p, :, peer(chips - e, 0)]
        return pltpu.make_async_remote_copy(
            src_ref=block, dst_ref=block, send_sem=h_send.at[p, e - 1], recv_sem=h_recv.at[p, e - 1],
            device_id=(pb, mate), device_id_type=MESH)

    def shed(p, s):
        to = peer(*order[s])
        return pltpu.make_async_remote_copy(
            src_ref=f2s.at[p, s], dst_ref=f2r.at[p, s], send_sem=s_send.at[p, s], recv_sem=s_recv.at[p, s],
            device_id=(pb, to), device_id_type=MESH)

    def c_rows(j):
        return pl.ds(pl.multiple_of(j * share, share), share)

    def own_c(p):
        return pltpu.make_async_copy(cbuf.at[p, c_rows(pb)], out.at[p, pb], c_recv.at[p, 0])

    def give(p, d):
        j = lax.rem(pb + d, pb_count)
        return pltpu.make_async_remote_copy(
            src_ref=cbuf.at[p, c_rows(j)], dst_ref=out.at[p, pb], send_sem=c_send.at[p, d], recv_sem=c_recv.at[p, d],
            device_id=(j, row), device_id_type=MESH)

    def loop(low, high, body):
        def step(i, c):
            body(i)
            return c
        lax.fori_loop(low, high, step, 0)

    def send_pair(p):
        own(p).start()
        loop(1, pb_count, lambda d: direct(p, d).start())

    loop(0, pair_total, send_pair)

    def spread(p):
        own(p).wait()
        loop(1, pb_count, lambda d: direct(p, d).wait_recv())
        for e in range(1, chips):
            across(p, e).start()
        to_mate(p).start()

    def pass_far(p):
        for e in range(1, chips):
            across(p, e).wait_recv()
            onward(p, e).start()

    low = lax.broadcasted_iota(jnp.int32, (row_count, lanes), 1) < width

    def finish_pair(p):
        total = f2s[p, row_devices - 1].astype(F32)
        for s in range(row_devices - 1):
            shed(p, s).wait_recv()
            total = total + f2r[p, s].astype(F32)
        stacked = jnp.concatenate([jnp.zeros_like(total), total], axis=0)
        cbuf[p] = jnp.where(low, f1[p], stacked.T).astype(BF16)
        loop(1, pb_count, lambda d: give(p, d).start())
        own_c(p).start()

    def tile_of(p, s):
        to = peer(*order[s])
        cols = pl.ds(pl.multiple_of(to * row_count, row_count), row_count)
        there = points(p, to)
        second = None
        chunk = row_count // 2
        for m in range(2):
            here = slice(m * chunk, (m + 1) * chunk)
            weight = w[here, cols].astype(F32)
            gram = lax.dot_general(rows_r[here], there, NT, preferred_element_type=F32)
            first = jnp.dot((weight * gram).astype(BF16), there, preferred_element_type=F32)
            f1[p, here] = first if s == 0 else f1[p, here] + first
            gram = lax.dot_general(rows_l[here], there, NT, preferred_element_type=F32)
            term = jnp.dot(rows_t[:, here], (weight * gram).astype(BF16), preferred_element_type=F32)
            second = term if second is None else second + term
        f2s[p, s] = second[width:].astype(BF16)
        if s < row_devices - 1:
            shed(p, s).start()

    spread(0)
    pass_far(0)
    w_copy.wait()

    def pair_step(p):
        to_mate(p).wait_recv()
        for e in range(1, chips):
            onward(p, e).wait_recv()
        mine = points(p, row).astype(F32)
        rows_r[...] = jnp.where(low, 0, mine).astype(BF16)
        rows_l[...] = jnp.where(low, mine, 0).astype(BF16)
        rows_t[...] = mine.T.astype(BF16)
        for s in range(row_devices):
            tile_of(p, s)
            if s == 0:
                pl.when(p + 1 < pair_total)(lambda: spread(p + 1))
                pl.when(p > 0)(lambda: finish_pair(p - 1))
            if s == row_devices - 2:
                pl.when(p + 1 < pair_total)(lambda: pass_far(p + 1))

    loop(0, pair_total, pair_step)
    finish_pair(pair_total - 1)

    def settle(p):
        own_c(p).wait()

        to_mate(p).wait_send()
        for e in range(1, chips):
            across(p, e).wait_send()
            onward(p, e).wait_send()

        def one(d):
            direct(p, d).wait_send()
            give(p, d).wait()

        loop(1, pb_count, one)
        for s in range(row_devices - 1):
            shed(p, s).wait_send()

    loop(0, pair_total, settle)


def combine_kernel(width, pairs_ref, count_ref, got_ref, out_ref):
    pair_total, pb_count, share, lanes = got_ref.shape
    low = lax.broadcasted_iota(jnp.int32, (share, lanes), 1) < width
    out_ref[...] = jnp.zeros_like(out_ref)

    def step(n, carry):
        q, p = lax.rem(n, pb_count), lax.div(n, pb_count)

        @pl.when(p < count_ref[q])
        def _():
            block = got_ref[p, q].astype(F32)
            moved = pltpu.roll(block, width, 1)
            for side in range(2):
                k = pairs_ref[q, p, side]
                odd = k & 1
                value = jnp.where(odd == side, block, moved)
                value = jnp.where(low == (odd == 0), value, 0.0)
                spot = pl.ds(pl.multiple_of((k >> 1) * lanes, lanes), lanes)
                out_ref[0, :, spot] += value

        return carry

    lax.fori_loop(0, pair_total * pb_count, step, 0)


def shards(kernels, orbitals, pairs, k_slot, pair_count):
    pb_count, row_devices = lax.axis_size("pb"), lax.axis_size("row")
    row_count, point_total = kernels.shape[1:]
    pair_total = pairs.shape[1]
    k_total = k_slot.shape[0]
    width = orbitals.shape[1] // k_total
    lanes = 2 * width
    piece = orbitals.shape[0] // row_devices
    far = max(row_devices // 2 - 1, 1)
    share = row_count // pb_count
    smem = pl.BlockSpec(memory_space=pltpu.SMEM)
    vmem = pl.BlockSpec(memory_space=pltpu.VMEM)
    hbm = pl.BlockSpec(memory_space=pl.ANY)
    picked = pl.pallas_call(
        functools.partial(pick_kernel, width),
        out_shape=jax.ShapeDtypeStruct((pair_total, pb_count, piece, lanes), BF16),
        in_specs=[smem, smem, vmem],
        out_specs=vmem,
    )(pairs, k_slot, orbitals)
    sems = pltpu.SemaphoreType.DMA
    got = pl.pallas_call(
        functools.partial(main_kernel, (pb_count, row_devices, pair_total, piece, width)),
        out_shape=jax.ShapeDtypeStruct((pair_total, pb_count, share, lanes), BF16),
        in_specs=[hbm, hbm],
        out_specs=hbm,
        scratch_shapes=[
            pltpu.VMEM((row_count, point_total), BF16),
            pltpu.VMEM((pair_total, pb_count, row_devices, piece, lanes), BF16),
            pltpu.VMEM((row_count, lanes), BF16),
            pltpu.VMEM((row_count, lanes), BF16),
            pltpu.VMEM((lanes, row_count), BF16),
            pltpu.VMEM((pair_total, row_count, lanes), F32),
            pltpu.VMEM((pair_total, row_devices, width, row_count), BF16),
            pltpu.VMEM((pair_total, row_devices, width, row_count), BF16),
            pltpu.VMEM((pair_total, row_count, lanes), BF16),
            sems,
            sems((pair_total, pb_count)),
            sems((pair_total, pb_count)),
            sems((pair_total,)),
            sems((pair_total,)),
            sems((pair_total, far)),
            sems((pair_total, far)),
            sems((pair_total, far)),
            sems((pair_total, far)),
            sems((pair_total, row_devices)),
            sems((pair_total, row_devices)),
            sems((pair_total, pb_count)),
            sems((pair_total, pb_count)),
        ],
        compiler_params=pltpu.CompilerParams(
            collective_id=0, has_side_effects=True, vmem_limit_bytes=56 * 1024 * 1024
        ),
    )(picked, kernels)
    return pl.pallas_call(
        functools.partial(combine_kernel, width),
        out_shape=jax.ShapeDtypeStruct((1, share, k_total * width), F32),
        in_specs=[smem, smem, vmem],
        out_specs=vmem,
    )(pairs, pair_count, got)


def solution(mesh):
    placed = (P("pb", "row", None), P("pb", None), P(), P(), P())
    return jax.shard_map(
        shards, mesh=mesh, in_specs=placed, out_specs=P("row", "pb", None), check_vma=False
    )
```

```python
import functools

import jax
import jax.numpy as jnp
from jax import lax
from jax.experimental import pallas as pl
from jax.experimental.pallas import tpu as pltpu
from jax.sharding import PartitionSpec as P

MESH = pl.DeviceIdType.MESH
BF16 = jnp.bfloat16
F32 = jnp.float32
NT = (((1,), (1,)), ((), ()))


def pick_kernel(width, pairs_ref, slot_ref, orb_ref, out_ref):
    pair_total, pb_count, piece, lanes = out_ref.shape
    rows = pl.ds(pl.multiple_of(lax.axis_index("row") * piece, piece), piece)
    low = lax.broadcasted_iota(jnp.int32, (piece, lanes), 1) < width

    def fetch(k, want):
        slot = slot_ref[k]
        block = orb_ref[rows, pl.ds(pl.multiple_of((slot >> 1) * lanes, lanes), lanes)].astype(F32)
        moved = pltpu.roll(block, width, 1)
        return jnp.where((slot & 1) == want, block, moved)

    def step(q, carry):
        for p in range(pair_total):
            left = fetch(pairs_ref[q, p, 0], 0)
            right = fetch(pairs_ref[q, p, 1], 1)
            out_ref[p, q] = jnp.where(low, left, right).astype(BF16)
        return carry

    lax.fori_loop(0, pb_count, step, 0)


def main_kernel(dims, picked, kern, out, w, basis, rows_r, rows_l, rows_t, f1, f2s, f2r, cbuf,
                w_sem, d_send, d_recv, g_send, g_recv, h_send, h_recv, y_send, y_recv,
                s_send, s_recv, c_send, c_recv):
    pb_count, row_devices, pair_total, piece, width = dims
    pb, row = lax.axis_index("pb"), lax.axis_index("row")
    chips = row_devices // 2
    part, chip = lax.rem(row, 2), lax.div(row, 2)
    mate = row + 1 - 2 * part
    row_count = w.shape[0]
    lanes = basis.shape[4]
    share = row_count // pb_count
    order = [(e, flip) for e in range(1, chips) for flip in (0, 1)] + [(0, 1), (0, 0)]

    def peer(e, flip):
        side = 1 - part if flip else part
        return 2 * lax.rem(chip + e, chips) + side

    w_copy = pltpu.make_async_copy(kern.at[0], w, w_sem)
    w_copy.start()

    barrier = pltpu.get_barrier_semaphore()

    def greet_pb(d, c):
        pl.semaphore_signal(barrier, inc=1, device_id=(lax.rem(pb + d, pb_count), row), device_id_type=MESH)
        return c

    def greet_row(d, c):
        pl.semaphore_signal(barrier, inc=1, device_id=(pb, lax.rem(row + d, row_devices)), device_id_type=MESH)
        return c

    lax.fori_loop(1, pb_count, greet_pb, 0)
    lax.fori_loop(1, row_devices, greet_row, 0)
    pl.semaphore_wait(barrier, pb_count + row_devices - 2)

    def spot(p, j, which):
        return basis.at[p, j, which]

    def points(p, r):
        span = pb_count // row_devices
        return basis[p, pl.ds(r * span, span)].reshape(row_count, lanes)

    def own(p):
        return pltpu.make_async_copy(picked.at[p, pb], spot(p, pb, row), d_recv.at[p, 0])

    def direct(p, d):
        q = lax.rem(pb + d, pb_count)
        return pltpu.make_async_remote_copy(
            src_ref=picked.at[p, q], dst_ref=spot(p, pb, row),
            send_sem=d_send.at[p, d], recv_sem=d_recv.at[p, d],
            device_id=(q, row), device_id_type=MESH)

    def across(p, e):
        block = basis.at[p, :, row]
        return pltpu.make_async_remote_copy(
            src_ref=block, dst_ref=block, send_sem=y_send.at[p, e - 1], recv_sem=y_recv.at[p, e - 1],
            device_id=(pb, peer(e, 0)), device_id_type=MESH)

    def to_mate(p):
        block = basis.at[p, :, row]
        return pltpu.make_async_remote_copy(
            src_ref=block, dst_ref=block, send_sem=g_send.at[p], recv_sem=g_recv.at[p],
            device_id=(pb, mate), device_id_type=MESH)

    def onward(p, e):
        block = basis.at[p, :, peer(chips - e, 0)]
        return pltpu.make_async_remote_copy(
            src_ref=block, dst_ref=block, send_sem=h_send.at[p, e - 1], recv_sem=h_recv.at[p, e - 1],
            device_id=(pb, mate), device_id_type=MESH)

    def shed(p, s):
        to = peer(*order[s])
        return pltpu.make_async_remote_copy(
            src_ref=f2s.at[p, s], dst_ref=f2r.at[p, s], send_sem=s_send.at[p, s], recv_sem=s_recv.at[p, s],
            device_id=(pb, to), device_id_type=MESH)

    def c_rows(j):
        return pl.ds(pl.multiple_of(j * share, share), share)

    def own_c(p):
        return pltpu.make_async_copy(cbuf.at[p, c_rows(pb)], out.at[p, pb], c_recv.at[p, 0])

    def give(p, d):
        j = lax.rem(pb + d, pb_count)
        return pltpu.make_async_remote_copy(
            src_ref=cbuf.at[p, c_rows(j)], dst_ref=out.at[p, pb], send_sem=c_send.at[p, d], recv_sem=c_recv.at[p, d],
            device_id=(j, row), device_id_type=MESH)

    def loop(low, high, body):
        def step(i, c):
            body(i)
            return c
        lax.fori_loop(low, high, step, 0)

    def send_pair(p):
        own(p).start()
        loop(1, pb_count, lambda d: direct(p, d).start())

    loop(0, pair_total, send_pair)

    def spread(p):
        own(p).wait()
        loop(1, pb_count, lambda d: direct(p, d).wait_recv())
        for e in range(1, chips):
            across(p, e).start()
        to_mate(p).start()

    def pass_far(p):
        for e in range(1, chips):
            across(p, e).wait_recv()
            onward(p, e).start()

    low = lax.broadcasted_iota(jnp.int32, (row_count, lanes), 1) < width

    def finish_pair(p):
        total = f2s[p, row_devices - 1].astype(F32)
        for s in range(row_devices - 1):
            shed(p, s).wait_recv()
            total = total + f2r[p, s].astype(F32)
        stacked = jnp.concatenate([jnp.zeros_like(total), total], axis=0)
        cbuf[p] = jnp.where(low, f1[p], stacked.T).astype(BF16)
        loop(1, pb_count, lambda d: give(p, d).start())
        own_c(p).start()

    def tile_of(p, s):
        to = peer(*order[s])
        cols = pl.ds(pl.multiple_of(to * row_count, row_count), row_count)
        there = points(p, to)
        second = None
        chunk = row_count // 2
        for m in range(2):
            here = slice(m * chunk, (m + 1) * chunk)
            weight = w[here, cols].astype(F32)
            gram = lax.dot_general(rows_r[here], there, NT, preferred_element_type=F32)
            first = jnp.dot((weight * gram).astype(BF16), there, preferred_element_type=F32)
            f1[p, here] = first if s == 0 else f1[p, here] + first
            gram = lax.dot_general(rows_l[here], there, NT, preferred_element_type=F32)
            term = jnp.dot(rows_t[:, here], (weight * gram).astype(BF16), preferred_element_type=F32)
            second = term if second is None else second + term
        f2s[p, s] = second[width:].astype(BF16)
        if s < row_devices - 1:
            shed(p, s).start()

    spread(0)
    pass_far(0)
    w_copy.wait()

    def pair_step(p):
        to_mate(p).wait_recv()
        for e in range(1, chips):
            onward(p, e).wait_recv()
        mine = points(p, row).astype(F32)
        rows_r[...] = jnp.where(low, 0, mine).astype(BF16)
        rows_l[...] = jnp.where(low, mine, 0).astype(BF16)
        rows_t[...] = mine.T.astype(BF16)
        for s in range(row_devices):
            tile_of(p, s)
            if s == 0:
                pl.when(p + 1 < pair_total)(lambda: spread(p + 1))
                pl.when(p > 0)(lambda: finish_pair(p - 1))
            if s == row_devices - 2:
                pl.when(p + 1 < pair_total)(lambda: pass_far(p + 1))

    loop(0, pair_total, pair_step)
    finish_pair(pair_total - 1)

    def settle(p):
        own_c(p).wait()

        to_mate(p).wait_send()
        for e in range(1, chips):
            across(p, e).wait_send()
            onward(p, e).wait_send()

        def one(d):
            direct(p, d).wait_send()
            give(p, d).wait()

        loop(1, pb_count, one)
        for s in range(row_devices - 1):
            shed(p, s).wait_send()

    loop(0, pair_total, settle)


def combine_kernel(width, pairs_ref, count_ref, got_ref, out_ref):
    pair_total, pb_count, share, lanes = got_ref.shape
    low = lax.broadcasted_iota(jnp.int32, (share, lanes), 1) < width
    out_ref[...] = jnp.zeros_like(out_ref)

    def step(q, carry):
        for p in range(pair_total):
            live = p < count_ref[q]
            block = jnp.where(live, got_ref[p, q].astype(F32), 0.0)
            moved = pltpu.roll(block, width, 1)
            for side in range(2):
                k = pairs_ref[q, p, side]
                odd = k & 1
                value = jnp.where(odd == side, block, moved)
                value = jnp.where(low == (odd == 0), value, 0.0)
                spot = pl.ds(pl.multiple_of((k >> 1) * lanes, lanes), lanes)
                out_ref[0, :, spot] += value
        return carry

    lax.fori_loop(0, pb_count, step, 0)


def shards(kernels, orbitals, pairs, k_slot, pair_count):
    pb_count, row_devices = lax.axis_size("pb"), lax.axis_size("row")
    row_count, point_total = kernels.shape[1:]
    pair_total = pairs.shape[1]
    k_total = k_slot.shape[0]
    width = orbitals.shape[1] // k_total
    lanes = 2 * width
    piece = orbitals.shape[0] // row_devices
    far = max(row_devices // 2 - 1, 1)
    share = row_count // pb_count
    smem = pl.BlockSpec(memory_space=pltpu.SMEM)
    vmem = pl.BlockSpec(memory_space=pltpu.VMEM)
    hbm = pl.BlockSpec(memory_space=pl.ANY)
    picked = pl.pallas_call(
        functools.partial(pick_kernel, width),
        out_shape=jax.ShapeDtypeStruct((pair_total, pb_count, piece, lanes), BF16),
        in_specs=[smem, smem, vmem],
        out_specs=vmem,
    )(pairs, k_slot, orbitals)
    sems = pltpu.SemaphoreType.DMA
    got = pl.pallas_call(
        functools.partial(main_kernel, (pb_count, row_devices, pair_total, piece, width)),
        out_shape=jax.ShapeDtypeStruct((pair_total, pb_count, share, lanes), BF16),
        in_specs=[hbm, hbm],
        out_specs=hbm,
        scratch_shapes=[
            pltpu.VMEM((row_count, point_total), BF16),
            pltpu.VMEM((pair_total, pb_count, row_devices, piece, lanes), BF16),
            pltpu.VMEM((row_count, lanes), BF16),
            pltpu.VMEM((row_count, lanes), BF16),
            pltpu.VMEM((lanes, row_count), BF16),
            pltpu.VMEM((pair_total, row_count, lanes), F32),
            pltpu.VMEM((pair_total, row_devices, width, row_count), BF16),
            pltpu.VMEM((pair_total, row_devices, width, row_count), BF16),
            pltpu.VMEM((pair_total, row_count, lanes), BF16),
            sems,
            sems((pair_total, pb_count)),
            sems((pair_total, pb_count)),
            sems((pair_total,)),
            sems((pair_total,)),
            sems((pair_total, far)),
            sems((pair_total, far)),
            sems((pair_total, far)),
            sems((pair_total, far)),
            sems((pair_total, row_devices)),
            sems((pair_total, row_devices)),
            sems((pair_total, pb_count)),
            sems((pair_total, pb_count)),
        ],
        compiler_params=pltpu.CompilerParams(
            collective_id=0, has_side_effects=True, vmem_limit_bytes=56 * 1024 * 1024
        ),
    )(picked, kernels)
    return pl.pallas_call(
        functools.partial(combine_kernel, width),
        out_shape=jax.ShapeDtypeStruct((1, share, k_total * width), F32),
        in_specs=[smem, smem, vmem],
        out_specs=vmem,
    )(pairs, pair_count, got)


def solution(mesh):
    placed = (P("pb", "row", None), P("pb", None), P(), P(), P())
    return jax.shard_map(
        shards, mesh=mesh, in_specs=placed, out_specs=P("row", "pb", None), check_vma=False
    )
```
